32 devices in a mesh: groups: 2 (over x), lat: 8 (over z, y), rep: 2 (over core).
Axes of the slice: x: 2, y: 2, z: 4, core: 2. Of those that a mesh axis runs over, the one named last changes fastest.
Arguments:
- acts: bfloat16 [128, 2304], P(('groups', 'lat', 'rep')), parts along dimension 0, may hold values from -6 to 6
- dest: int32 [128], P(('groups', 'lat', 'rep')), parts along dimension 0, may hold values from 0 to 7, as said below
- counts: int32 [32], P(('groups', 'lat', 'rep')), parts along dimension 0, may hold values from 2 to 4, as said below
- w_gate: bfloat16 [2304, 9216], P(None, 'lat'), may hold values from -0.125 to 0.125
- w_up: bfloat16 [2304, 9216], P(None, 'lat'), may hold values from -0.125 to 0.125
- w_down: bfloat16 [9216, 2304], P('lat'), may hold values from -0.0625 to 0.0625
- enc_weight: float32 [2, 2304, 16384], P('rep', None, 'lat'), may hold values from -0.125 to 0.125
- enc_bias: float32 [2, 16384], P('rep', 'lat'), may hold values from -1.5 to 1.5
- dec_weight: float32 [2, 16384, 2304], P('rep', 'lat'), may hold values from -0.09375 to 0.09375
- dec_bias: float32 [2, 2304], P('rep'), may hold values from -3 to 3
Outputs:
- grad_dec: float32 [4, 16384, 2304], P(('groups', 'rep'), 'lat'), parts along dimension 0
The draws below stay inside these ranges and needn't reach their ends.
There are 2 independent parts, one for each index of `groups`. The reference program is written for one: setup_inputs(seed, part) draws one part's arguments, and reference() takes and returns one part's arrays. A program takes and returns all parts, laid end to end along the dimension named above; an argument that names none is the same for every part. Nothing has to cross between parts.
Inputs may be any that keep to these rules, and one draw needn't show every extreme that they name: `dest`: Micro-batch m belongs to autoencoder m // 4. Of the valid rows held by the two devices of one lat index (row blocks 2l and 2l + 1), at most 6 go to each autoencoder; in every draw some lat index sends exactly 6 to autoencoder 0 and another exactly 6 to autoencoder 1. Every micro-batch holds at least one valid row. Entries of rows that are not valid carry no meaning. The valid rows of a block are its first counts[k] rows.
All inputs are finite; a program needn't handle non-finite values.
Results may differ from the reference program's by a relative error of at most 0.0029.
Values may be sent and summed in bfloat16 or wider, within the bound.
No kernel may reach another device: no remote copies, remote signals or barrier semaphores. Data moves between devices by JAX's collectives and lax.ppermute only.
A program may use at most 128 MiB of HBM per device.

```python
import jax
import jax.numpy as jnp
from jax import lax

D = 2304
FF = 9216
LATENTS = 16384
ROW_DEV = 4
MB_REP = 4
CAP = 6
ROWS = 64
N_LAT = 8
N_REP = 2


def shuffle_plan(key):
    base = jax.random.fold_in(key, 11)
    keys = jax.random.split(base, 7)
    slot_count = 2 * ROW_DEV
    block_counts = jax.random.randint(keys[0], (N_LAT, 2), ROW_DEV // 2, ROW_DEV + 1)
    first = jax.random.randint(keys[1], (), 0, N_LAT)
    second = (first + 1 + jax.random.randint(keys[2], (), 0, N_LAT - 1)) % N_LAT
    lane = jnp.arange(N_LAT)
    forced = (lane == first) | (lane == second)
    block_counts = jnp.where(forced[:, None], ROW_DEV, block_counts)
    total = jnp.sum(block_counts, axis=1)
    lower = jnp.maximum(total - CAP, 0)
    upper = jnp.minimum(total, CAP)
    to_first_count = jax.random.randint(keys[3], (N_LAT,), lower, upper + 1)
    to_first_count = jnp.where(lane == first, CAP, jnp.where(lane == second, 2 * ROW_DEV - CAP, to_first_count))
    slots = jnp.arange(slot_count)
    position = slots % ROW_DEV
    side = slots // ROW_DEV
    valid = position[None, :] < block_counts[:, side]
    score = jax.random.randint(keys[4], (N_LAT, slot_count), 0, 1 << 20) * slot_count + slots[None, :]
    score = score + jnp.where(valid, 0, 1 << 27)
    ranking = jnp.argsort(jnp.argsort(score, axis=1), axis=1)
    to_first = ranking < to_first_count[:, None]
    replica = jnp.where(to_first, 0, 1)
    random_sub = jnp.minimum(jax.random.randint(keys[5], (N_LAT, slot_count), 0, MB_REP), jax.random.randint(keys[6], (N_LAT, slot_count), 0, MB_REP))
    cyclic_sub = jnp.where(to_first, ranking, ranking - to_first_count[:, None]) % MB_REP
    sub_batch = jnp.where(forced[:, None], cyclic_sub, random_sub)
    dest_rows = (replica * MB_REP + sub_batch).reshape(N_LAT * slot_count)
    return (dest_rows.astype(jnp.int32), block_counts.reshape(N_LAT * N_REP).astype(jnp.int32))


def draw_dest(key, part):
    return shuffle_plan(key)[0]


def draw_counts(key, part):
    return shuffle_plan(key)[1]


def levels(own_key, extent, pieces, low, high):
    loudness, own = 1.0, jax.random.fold_in(own_key, 6)
    for axis_at, parts in pieces:
        draws = jnp.exp(jax.random.uniform(jax.random.fold_in(own, axis_at), (parts,), jnp.float32, low / len(pieces), high / len(pieces)))
        loudness = loudness * jnp.repeat(draws, extent[axis_at] // parts).reshape([-1 if axis == axis_at else 1 for axis in range(len(extent))])
    return loudness


def bell_draw(stream_key, extent, deviation, limit, shards=(), kind=jnp.bfloat16):
    values = jax.random.normal(stream_key, extent, jnp.float32) * deviation
    if len(shards) > 0:
        values = levels(stream_key, extent, shards, -0.22, 0.18) * values
    return jnp.clip(values, min=-limit, max=limit).astype(kind)


def setup_inputs(seed: int = 0, part: int = 0) -> dict:
    seeds = jax.random.split(jax.random.key(seed), 11)
    own_keys = jax.random.split(jax.random.fold_in(seeds[10], part), 11)
    return {
        "acts": bell_draw(own_keys[0], (ROWS, D), 1.0, 6.0, ((0, 16),)),
        "dest": draw_dest(jax.random.fold_in(jax.random.fold_in(seeds[10], part), 71), part),
        "counts": draw_counts(jax.random.fold_in(jax.random.fold_in(seeds[10], part), 71), part),
        "w_gate": bell_draw(seeds[3], (D, FF), D ** -0.5, 0.125, ((1, 8),)),
        "w_up": bell_draw(seeds[4], (D, FF), D ** -0.5, 0.125, ((1, 8),)),
        "w_down": bell_draw(seeds[5], (FF, D), FF ** -0.5, 0.0625, ((0, 8),)),
        "enc_weight": bell_draw(seeds[6], (N_REP, D, LATENTS), D ** -0.5, 0.125, ((0, 2), (2, 8)), jnp.float32),
        "enc_bias": bell_draw(seeds[7], (N_REP, LATENTS), 0.3, 1.5, ((0, 2), (1, 8)), jnp.float32),
        "dec_weight": bell_draw(seeds[8], (N_REP, LATENTS, D), (LATENTS // 4) ** -0.5, 0.09375, ((0, 2), (1, 8)), jnp.float32),
        "dec_bias": bell_draw(seeds[9], (N_REP, D), 0.5, 3.0, ((0, 2),), jnp.float32),
    }


def reference(acts, dest, counts, w_gate, w_up, w_down, enc_weight, enc_bias, dec_weight, dec_bias):
    gate = jnp.dot(acts, w_gate, preferred_element_type=jnp.float32)
    up = jnp.dot(acts, w_up, preferred_element_type=jnp.float32)
    hidden = (jax.nn.gelu(gate, approximate=True) * up).astype(jnp.bfloat16)
    feats = jnp.dot(hidden, w_down, preferred_element_type=jnp.float32).astype(jnp.bfloat16)
    row_ids = jnp.arange(ROWS, dtype=jnp.int32)
    block_ids = row_ids // ROW_DEV
    position = row_ids % ROW_DEV
    valid = position < counts[block_ids]
    batches = jnp.arange(N_REP * MB_REP, dtype=jnp.int32)
    member = ((dest[:, None] == batches[None, :]) & valid[:, None]).astype(jnp.float32)
    sizes = jnp.sum(member, axis=0)
    safe_sizes = jnp.where(sizes > 0.0, sizes, 1.0)
    weight = jnp.sum(member / safe_sizes[None, :], axis=1)
    replica_of = dest // MB_REP
    feats_wide = feats.astype(jnp.float32)
    results = []
    for replica in range(N_REP):
        row_weight = jnp.where(replica_of == replica, weight, 0.0)
        pre = jnp.dot(feats_wide, enc_weight[replica], precision=lax.Precision.HIGHEST, preferred_element_type=jnp.float32) + enc_bias[replica]
        codes = jnp.maximum(pre, 0.0)
        recon = jnp.dot(codes, dec_weight[replica], precision=lax.Precision.HIGHEST, preferred_element_type=jnp.float32) + dec_bias[replica]
        err = recon - feats_wide
        scaled = 2.0 * row_weight[:, None] * err
        grad = lax.dot_general(codes, scaled, (((0,), (0,)), ((), ())), precision=lax.Precision.HIGHEST, preferred_element_type=jnp.float32)
        results.append(grad)
    return jnp.stack(results)
```

```python
import functools

import jax
import jax.numpy as jnp
from jax import lax
from jax.experimental import pallas as pl
from jax.experimental.pallas import tpu as pltpu
from jax.sharding import PartitionSpec as P

MB_REP = 4
CAP = 6
SUB = 8
LANE = 128
BF = jnp.bfloat16
F4 = jnp.float32
CODER_BYTES = 46 << 20
GRAD_BYTES = 26 << 20


def dot(a, b):
    return jnp.dot(a, b, preferred_element_type=F4)


def split(x):
    high = x.astype(BF)
    return high, (x - high.astype(F4)).astype(BF)


def chunk_rows(extent, want):
    return want if extent % want == 0 else extent


def mlp_kernel(step, down_step, piece, gate_hbm, up_hbm, down_hbm, out, gate_v, up_v, down_v, gate_acc, up_acc, sems):
    depth, hidden_n = gate_v.shape
    width = down_v.shape[1]
    n, row_dev = piece.shape[:2]
    rows = n * row_dev
    copies = []
    for k in range(depth // step):
        part = pl.ds(k * step, step)
        copies.append(
            (
                pltpu.make_async_copy(gate_hbm.at[part], gate_v.at[part], sems.at[2 * k]),
                pltpu.make_async_copy(up_hbm.at[part], up_v.at[part], sems.at[2 * k + 1]),
            )
        )
    base = 2 * (depth // step)
    downs = []
    for k in range(hidden_n // down_step):
        part = pl.ds(k * down_step, down_step)
        downs.append(pltpu.make_async_copy(down_hbm.at[part], down_v.at[part], sems.at[base + k]))
    for pair in copies:
        pair[0].start()
        pair[1].start()
    for copy in downs:
        copy.start()
    whole = jnp.concatenate([piece[s].astype(F4) for s in range(n)], axis=0).astype(BF)
    for k, pair in enumerate(copies):
        part = pl.ds(k * step, step)
        left = whole[:, k * step : (k + 1) * step]
        pair[0].wait()
        gate_part = dot(left, gate_v[part, :])
        pair[1].wait()
        up_part = dot(left, up_v[part, :])
        if k == 0:
            gate_acc[...] = gate_part
            up_acc[...] = up_part
        else:
            gate_acc[...] += gate_part
            up_acc[...] += up_part
    hidden = (jax.nn.gelu(gate_acc[...], approximate=True) * up_acc[...]).astype(BF)
    total = None
    for k, copy in enumerate(downs):
        copy.wait()
        part = dot(hidden[:, k * down_step : (k + 1) * down_step], down_v[pl.ds(k * down_step, down_step), :])
        total = part if total is None else total + part
    across = width // LANE
    share = out.shape[1]
    for t in range(rows // SUB * across):
        g, j = divmod(t, across)
        out[t // share, t % share] = total[g * SUB : (g + 1) * SUB, j * LANE : (j + 1) * LANE]


def coder_kernel(
    rows_side, step, down_step,
    own, other, biases, enc_hbm, dec_hbm,
    partial, codes_out,
    enc_v, dec_v, feats, acc, recon, sems,
):
    depth, latents = enc_v.shape
    width = dec_v.shape[1]
    across = width // LANE
    slots = acc.shape[0]
    encs, decs = [], []
    for k in range(depth // step):
        part = pl.ds(k * step, step)
        encs.append(pltpu.make_async_copy(enc_hbm.at[0, part], enc_v.at[part], sems.at[k]))
    for k in range(latents // down_step):
        part = pl.ds(k * down_step, down_step)
        decs.append(pltpu.make_async_copy(dec_hbm.at[0, part], dec_v.at[part], sems.at[len(encs) + k]))
    for copy in encs + decs:
        copy.start()

    share = own.shape[1] - 1
    labels = []
    for side, source in enumerate((own, other)):
        for g in range(rows_side // SUB):
            labels.append(source[2 * g, share].astype(F4) + source[2 * g + 1, share].astype(F4))
            for j in range(across):
                t = g * across + j
                feats[side * rows_side + g * SUB : side * rows_side + (g + 1) * SUB, j * LANE : (j + 1) * LANE] = source[t // share, t % share].astype(F4)
    label = jnp.concatenate(labels, axis=0)
    every = label.shape[0]
    first = (lax.axis_index("rep") * MB_REP).astype(F4) + 1.0
    keep = jnp.where((label >= first) & (label < first + MB_REP), 1.0, 0.0)
    row_of = lax.broadcasted_iota(jnp.int32, (every, every), 0)
    column_of = lax.broadcasted_iota(jnp.int32, (every, every), 1)
    keep_wide = jnp.broadcast_to(keep[:, :1], (every, every))
    keep_row = jnp.sum(jnp.where(row_of == column_of, keep_wide, 0.0), axis=0, keepdims=True)
    before = jnp.sum(jnp.where(row_of < column_of, keep_wide, 0.0), axis=0, keepdims=True)
    slot_of = lax.broadcasted_iota(jnp.int32, (slots, every), 0).astype(F4)
    picked = jnp.where((before == slot_of) & (keep_row > 0.0), 1.0, 0.0).astype(BF)
    slot_label = dot(picked, label.astype(BF))
    weight = jnp.zeros_like(slot_label)
    for m in range(MB_REP):
        size = jnp.sum(jnp.where(label == first + m, 1.0, 0.0), axis=0, keepdims=True)
        weight = weight + jnp.where(slot_label == first + m, 1.0 / jnp.maximum(size, 1.0), 0.0)
    twice = 2.0 * weight[:, :1]
    batch = dot(picked, feats[...].astype(BF))
    feats[0:slots, :] = batch

    for k, copy in enumerate(encs):
        left = batch[:, k * step : (k + 1) * step].astype(BF)
        copy.wait()
        high, low = split(enc_v[pl.ds(k * step, step), :])
        part = dot(left, high) + dot(left, low)
        if k == 0:
            acc[...] = part + biases[:, :latents]
        else:
            acc[...] += part
    codes = jnp.maximum(acc[...], 0.0)
    code_high, code_low = split(codes)
    out_high, out_low = split(twice * codes)
    codes_out[0:slots, :] = out_high
    codes_out[slots : 2 * slots, :] = out_low
    stacked = jnp.concatenate([code_high, code_low], axis=0)
    for k, copy in enumerate(decs):
        part = slice(k * down_step, (k + 1) * down_step)
        copy.wait()
        high, low = split(dec_v[pl.ds(k * down_step, down_step), :])
        both = dot(stacked[:, part], high)
        here = both[:slots] + both[slots:] + dot(code_high[:, part], low)
        if k == 0:
            recon[...] = here
        else:
            recon[...] += here
    leads = lax.axis_index("lat") == 0
    local = recon[...] + jnp.where(leads, biases[:, latents:] - feats[0:slots, :], 0.0)
    out_share = partial.shape[1]
    tiles = slots // SUB * across
    for t in range(partial.shape[0] * out_share):
        if t < tiles:
            g, j = divmod(t, across)
            partial[t // out_share, t % out_share] = local[g * SUB : (g + 1) * SUB, j * LANE : (j + 1) * LANE]
        else:
            partial[t // out_share, t % out_share] = jnp.zeros((SUB, LANE), F4)


def grad_kernel(block, err, codes, out, stacked, held, sems):
    slots = stacked.shape[0] // 2
    latents, width = held.shape
    across = width // LANE
    share = err.shape[1]
    for t in range(slots // SUB * across):
        g, j = divmod(t, across)
        tile = err[t // share, t % share]
        for half in (0, slots):
            stacked[half + g * SUB : half + (g + 1) * SUB, j * LANE : (j + 1) * LANE] = tile
    copies = []
    for k in range(latents // block):
        part = pl.ds(k * block, block)
        held[part, :] = lax.dot_general(
            codes[:, k * block : (k + 1) * block], stacked[...], (((0,), (0,)), ((), ())), preferred_element_type=F4
        )
        copies.append(pltpu.make_async_copy(held.at[part], out.at[0, part], sems.at[k]))
        copies[-1].start()
    for copy in copies:
        copy.wait()


def exchange(blocks):
    return lax.all_to_all(blocks, "lat", 0, 0)


def to_all(block, n):
    return exchange(jnp.broadcast_to(block[None], (n, *block.shape)))


def shards(acts, dest, counts, w_gate, w_up, w_down, enc_weight, enc_bias, dec_weight, dec_bias):
    n = lax.axis_size("lat")
    row_dev, depth = acts.shape
    hidden_n = w_gate.shape[1]
    width = w_down.shape[1]
    latents = enc_weight.shape[2]
    across = width // LANE
    rows = n * row_dev
    share = rows // SUB * across // n
    slots = n * CAP
    out_share = pl.cdiv(slots // SUB * across, n)
    anywhere = pl.BlockSpec(memory_space=pl.ANY)
    in_vmem = pl.BlockSpec(memory_space=pltpu.VMEM)

    piece = to_all(acts, n)
    step, down_step = chunk_rows(depth, 768), chunk_rows(hidden_n, 128)
    summed = pl.pallas_call(
        functools.partial(mlp_kernel, step, down_step),
        out_shape=jax.ShapeDtypeStruct((n, share, SUB, LANE), F4),
        in_specs=[in_vmem, anywhere, anywhere, anywhere],
        out_specs=in_vmem,
        scratch_shapes=[
            pltpu.VMEM((depth, hidden_n), BF),
            pltpu.VMEM((depth, hidden_n), BF),
            pltpu.VMEM((hidden_n, width), BF),
            pltpu.VMEM((rows, hidden_n), F4),
            pltpu.VMEM((rows, hidden_n), F4),
            pltpu.SemaphoreType.DMA((2 * (depth // step) + hidden_n // down_step,)),
        ],
        name="mlp",
    )(piece, w_gate, w_up, w_down)
    feats = jnp.sum(exchange(summed), axis=0).astype(BF)

    spot = jnp.arange(SUB, dtype=jnp.int32) - (lax.axis_index("lat") * row_dev) % SUB
    here = jnp.arange(row_dev, dtype=jnp.int32)
    tags = jnp.where(here < counts[0], dest + 1, 0)
    mark = jnp.sum(jnp.where(spot[:, None] == here[None, :], tags[None, :], 0), axis=1)
    mark = jnp.broadcast_to(mark[:, None], (SUB, LANE)).astype(BF)
    own = to_all(jnp.concatenate([feats, mark[None]], axis=0), n)
    other = lax.ppermute(own, "rep", [(0, 1), (1, 0)])

    step, down_step = chunk_rows(depth, 256), chunk_rows(latents, 256)
    partial, codes = pl.pallas_call(
        functools.partial(coder_kernel, rows, step, down_step),
        out_shape=(
            jax.ShapeDtypeStruct((n, out_share, SUB, LANE), F4),
            jax.ShapeDtypeStruct((2 * slots, latents), BF),
        ),
        in_specs=[in_vmem, in_vmem, in_vmem, anywhere, anywhere],
        out_specs=(in_vmem, in_vmem),
        scratch_shapes=[
            pltpu.VMEM((depth, latents), F4),
            pltpu.VMEM((latents, width), F4),
            pltpu.VMEM((2 * rows, width), F4),
            pltpu.VMEM((slots, latents), F4),
            pltpu.VMEM((slots, width), F4),
            pltpu.SemaphoreType.DMA((depth // step + latents // down_step,)),
        ],
        compiler_params=pltpu.CompilerParams(vmem_limit_bytes=CODER_BYTES),
        name="coder",
    )(own, other, jnp.concatenate([enc_bias, dec_bias], axis=1), enc_weight, dec_weight)
    err = to_all(jnp.sum(exchange(partial), axis=0).astype(BF), n)

    block = chunk_rows(latents, 128)
    return pl.pallas_call(
        functools.partial(grad_kernel, block),
        out_shape=jax.ShapeDtypeStruct((1, latents, width), F4),
        in_specs=[in_vmem, in_vmem],
        out_specs=anywhere,
        scratch_shapes=[
            pltpu.VMEM((2 * slots, width), BF),
            pltpu.VMEM((latents, width), F4),
            pltpu.SemaphoreType.DMA((latents // block,)),
        ],
        compiler_params=pltpu.CompilerParams(vmem_limit_bytes=GRAD_BYTES),
        name="grad",
    )(err, codes)


def solution(mesh):
    placed = (
        P(("groups", "lat", "rep"), None),
        P(("groups", "lat", "rep")),
        P(("groups", "lat", "rep")),
        P(None, "lat"),
        P(None, "lat"),
        P("lat", None),
        P("rep", None, "lat"),
        P("rep", "lat"),
        P("rep", "lat", None),
        P("rep", None),
    )
    return jax.shard_map(
        shards,
        mesh=mesh,
        in_specs=placed,
        out_specs=P(("groups", "rep"), "lat", None),
        check_vma=False,
    )
```

```python
import functools

import jax
import jax.numpy as jnp
from jax import lax
from jax.experimental import pallas as pl
from jax.experimental.pallas import tpu as pltpu
from jax.sharding import PartitionSpec as P

MB_REP = 4
CAP = 6
SUB = 8
LANE = 128
LIMIT = 32767.0
BF = jnp.bfloat16
F4 = jnp.float32
CODER_BYTES = 46 << 20
GRAD_BYTES = 26 << 20
GLUE_BYTES = 2 << 20


def dot(a, b):
    return jnp.dot(a, b, preferred_element_type=F4)


def split(x):
    high = x.astype(BF)
    return high, (x - high.astype(F4)).astype(BF)


def chunk_rows(extent, want):
    return want if extent % want == 0 else extent


def encode(local, out):
    share = out.shape[1] - 1
    across = local.shape[1] // LANE
    groups = local.shape[0] // SUB
    peak = jnp.max(jnp.abs(local), axis=1, keepdims=True)
    power = jnp.clip(jnp.ceil(jnp.log2(jnp.maximum(peak, 1e-30))), -96.0, 120.0)
    codes = jnp.clip(jnp.round(local * jnp.exp2(15.0 - power)), -LIMIT, LIMIT).astype(jnp.int32)
    lane = lax.broadcasted_iota(jnp.int32, (SUB, LANE), 1)
    powers = jnp.zeros((SUB, LANE), F4)
    for g in range(groups):
        powers = jnp.where(lane == g, power[g * SUB : (g + 1) * SUB], powers)
    powers = powers.astype(jnp.int32).astype(jnp.int16)
    for t in range(out.shape[0] * share):
        if t < groups * across:
            g, j = divmod(t, across)
            out[t // share, t % share] = codes[g * SUB : (g + 1) * SUB, j * LANE : (j + 1) * LANE].astype(jnp.int16)
        else:
            out[t // share, t % share] = jnp.zeros((SUB, LANE), jnp.int16)
    for s in range(out.shape[0]):
        out[s, share] = powers


def decode(parts, across):
    n, share = parts.shape[0], parts.shape[1] - 1
    start = lax.axis_index("lat") * share
    first = lax.div(start, across)
    lane = lax.broadcasted_iota(jnp.int32, (SUB, LANE), 1)
    units = []
    for s in range(n):
        scale = jnp.exp2(parts[s, share].astype(jnp.int32).astype(F4) - 15.0)
        units.append(
            [
                jnp.broadcast_to(jnp.sum(jnp.where(lane == first + h, scale, 0.0), axis=1, keepdims=True), (SUB, LANE))
                for h in range((share + across - 2) // across + 1)
            ]
        )
    tiles = []
    for t in range(share):
        ahead = lax.div(start + t, across) - first
        total = None
        for s in range(n):
            unit = units[s][0]
            for h in range(1, len(units[s])):
                unit = jnp.where(ahead == h, units[s][h], unit)
            value = parts[s, t].astype(jnp.int32).astype(F4) * unit
            total = value if total is None else total + value
        tiles.append(total.astype(BF))
    return tiles


def feats_kernel(across, row_dev, parts, mark, out):
    tiles = decode(parts, across)
    turn = lax.broadcasted_iota(jnp.int32, (SUB, LANE), 0) // row_dev
    mine = turn == lax.rem(lax.axis_index("lat"), SUB // row_dev)
    tags = jnp.where(mine, mark[...], 0.0).astype(BF)
    for s in range(parts.shape[0]):
        for t, tile in enumerate(tiles):
            out[s, t] = tile
        out[s, len(tiles)] = tags


def err_kernel(across, parts, out):
    tiles = decode(parts, across)
    for s in range(parts.shape[0]):
        for t, tile in enumerate(tiles):
            out[s, t] = tile


def mlp_kernel(step, down_step, piece, gate_hbm, up_hbm, down_hbm, out, gate_v, up_v, down_v, gate_acc, up_acc, sems):
    depth, hidden_n = gate_v.shape
    n = piece.shape[0]
    copies = []
    for k in range(depth // step):
        part = pl.ds(k * step, step)
        copies.append(
            (
                pltpu.make_async_copy(gate_hbm.at[part], gate_v.at[part], sems.at[2 * k]),
                pltpu.make_async_copy(up_hbm.at[part], up_v.at[part], sems.at[2 * k + 1]),
            )
        )
    base = 2 * (depth // step)
    downs = []
    for k in range(hidden_n // down_step):
        part = pl.ds(k * down_step, down_step)
        downs.append(pltpu.make_async_copy(down_hbm.at[part], down_v.at[part], sems.at[base + k]))
    for pair in copies:
        pair[0].start()
        pair[1].start()
    for copy in downs:
        copy.start()
    whole = jnp.concatenate([piece[s].astype(F4) for s in range(n)], axis=0).astype(BF)
    for k, pair in enumerate(copies):
        part = pl.ds(k * step, step)
        left = whole[:, k * step : (k + 1) * step]
        pair[0].wait()
        gate_part = dot(left, gate_v[part, :])
        pair[1].wait()
        up_part = dot(left, up_v[part, :])
        if k == 0:
            gate_acc[...] = gate_part
            up_acc[...] = up_part
        else:
            gate_acc[...] += gate_part
            up_acc[...] += up_part
    hidden = (jax.nn.gelu(gate_acc[...], approximate=True) * up_acc[...]).astype(BF)
    total = None
    for k, copy in enumerate(downs):
        copy.wait()
        part = dot(hidden[:, k * down_step : (k + 1) * down_step], down_v[pl.ds(k * down_step, down_step), :])
        total = part if total is None else total + part
    encode(total, out)


def coder_kernel(
    rows_side, step, down_step,
    own, other, biases, enc_hbm, dec_hbm,
    partial, codes_out,
    enc_v, dec_v, feats, acc, recon, sems,
):
    depth, latents = enc_v.shape
    width = dec_v.shape[1]
    across = width // LANE
    slots = acc.shape[0]
    encs, decs = [], []
    for k in range(depth // step):
        part = pl.ds(k * step, step)
        encs.append(pltpu.make_async_copy(enc_hbm.at[0, part], enc_v.at[part], sems.at[k]))
    for k in range(latents // down_step):
        part = pl.ds(k * down_step, down_step)
        decs.append(pltpu.make_async_copy(dec_hbm.at[0, part], dec_v.at[part], sems.at[len(encs) + k]))
    for copy in encs + decs:
        copy.start()

    share = own.shape[1] - 1
    labels = []
    for side, source in enumerate((own, other)):
        for g in range(rows_side // SUB):
            labels.append(source[2 * g, share].astype(F4) + source[2 * g + 1, share].astype(F4))
            for j in range(across):
                t = g * across + j
                feats[side * rows_side + g * SUB : side * rows_side + (g + 1) * SUB, j * LANE : (j + 1) * LANE] = source[t // share, t % share].astype(F4)
    label = jnp.concatenate(labels, axis=0)
    every = label.shape[0]
    first = (lax.axis_index("rep") * MB_REP).astype(F4) + 1.0
    keep = jnp.where((label >= first) & (label < first + MB_REP), 1.0, 0.0)
    row_of = lax.broadcasted_iota(jnp.int32, (every, every), 0)
    column_of = lax.broadcasted_iota(jnp.int32, (every, every), 1)
    keep_wide = jnp.broadcast_to(keep[:, :1], (every, every))
    keep_row = jnp.sum(jnp.where(row_of == column_of, keep_wide, 0.0), axis=0, keepdims=True)
    before = jnp.sum(jnp.where(row_of < column_of, keep_wide, 0.0), axis=0, keepdims=True)
    slot_of = lax.broadcasted_iota(jnp.int32, (slots, every), 0).astype(F4)
    picked = jnp.where((before == slot_of) & (keep_row > 0.0), 1.0, 0.0).astype(BF)
    slot_label = dot(picked, label.astype(BF))
    weight = jnp.zeros_like(slot_label)
    for m in range(MB_REP):
        size = jnp.sum(jnp.where(label == first + m, 1.0, 0.0), axis=0, keepdims=True)
        weight = weight + jnp.where(slot_label == first + m, 1.0 / jnp.maximum(size, 1.0), 0.0)
    twice = 2.0 * weight[:, :1]
    batch = dot(picked, feats[...].astype(BF))
    feats[0:slots, :] = batch

    for k, copy in enumerate(encs):
        left = batch[:, k * step : (k + 1) * step].astype(BF)
        copy.wait()
        high, low = split(enc_v[pl.ds(k * step, step), :])
        part = dot(left, high) + dot(left, low)
        if k == 0:
            acc[...] = part + biases[:, :latents]
        else:
            acc[...] += part
    codes = jnp.maximum(acc[...], 0.0)
    code_high, code_low = split(codes)
    out_high, out_low = split(twice * codes)
    codes_out[0:slots, :] = out_high
    codes_out[slots : 2 * slots, :] = out_low
    stacked = jnp.concatenate([code_high, code_low], axis=0)
    for k, copy in enumerate(decs):
        part = slice(k * down_step, (k + 1) * down_step)
        copy.wait()
        high, low = split(dec_v[pl.ds(k * down_step, down_step), :])
        both = dot(stacked[:, part], high)
        here = both[:slots] + both[slots:] + dot(code_high[:, part], low)
        if k == 0:
            recon[...] = here
        else:
            recon[...] += here
    leads = lax.axis_index("lat") == 0
    local = recon[...] + jnp.where(leads, biases[:, latents:] - feats[0:slots, :], 0.0)
    encode(local, partial)


def grad_kernel(block, err, codes, out, stacked, held, sems):
    slots = stacked.shape[0] // 2
    latents, width = held.shape
    across = width // LANE
    share = err.shape[1]
    for t in range(slots // SUB * across):
        g, j = divmod(t, across)
        tile = err[t // share, t % share]
        for half in (0, slots):
            stacked[half + g * SUB : half + (g + 1) * SUB, j * LANE : (j + 1) * LANE] = tile
    copies = []
    for k in range(latents // block):
        part = pl.ds(k * block, block)
        held[part, :] = lax.dot_general(
            codes[:, k * block : (k + 1) * block], stacked[...], (((0,), (0,)), ((), ())), preferred_element_type=F4
        )
        copies.append(pltpu.make_async_copy(held.at[part], out.at[0, part], sems.at[k]))
        copies[-1].start()
    for copy in copies:
        copy.wait()


def exchange(blocks):
    return lax.all_to_all(blocks, "lat", 0, 0)


def to_all(block, n):
    return exchange(jnp.broadcast_to(block[None], (n, *block.shape)))


def shards(acts, dest, counts, w_gate, w_up, w_down, enc_weight, enc_bias, dec_weight, dec_bias):
    n = lax.axis_size("lat")
    row_dev, depth = acts.shape
    hidden_n = w_gate.shape[1]
    width = w_down.shape[1]
    latents = enc_weight.shape[2]
    across = width // LANE
    rows = n * row_dev
    share = rows // SUB * across // n
    slots = n * CAP
    out_share = pl.cdiv(slots // SUB * across, n)
    anywhere = pl.BlockSpec(memory_space=pl.ANY)
    in_vmem = pl.BlockSpec(memory_space=pltpu.VMEM)

    piece = to_all(acts, n)
    step, down_step = chunk_rows(depth, 768), chunk_rows(hidden_n, 128)
    summed = pl.pallas_call(
        functools.partial(mlp_kernel, step, down_step),
        out_shape=jax.ShapeDtypeStruct((n, share + 1, SUB, LANE), jnp.int16),
        in_specs=[in_vmem, anywhere, anywhere, anywhere],
        out_specs=in_vmem,
        scratch_shapes=[
            pltpu.VMEM((depth, hidden_n), BF),
            pltpu.VMEM((depth, hidden_n), BF),
            pltpu.VMEM((hidden_n, width), BF),
            pltpu.VMEM((rows, hidden_n), F4),
            pltpu.VMEM((rows, hidden_n), F4),
            pltpu.SemaphoreType.DMA((2 * (depth // step) + hidden_n // down_step,)),
        ],
        name="mlp",
    )(piece, w_gate, w_up, w_down)
    parts = exchange(summed)

    tags = jnp.where(jnp.arange(row_dev, dtype=jnp.int32) < counts[0], dest + 1, 0)
    mark = jnp.broadcast_to(jnp.tile(tags, SUB // row_dev)[:, None], (SUB, LANE)).astype(F4)
    own = exchange(
        pl.pallas_call(
            functools.partial(feats_kernel, across, row_dev),
            out_shape=jax.ShapeDtypeStruct((n, share + 1, SUB, LANE), BF),
            in_specs=[in_vmem, in_vmem],
            out_specs=in_vmem,
            compiler_params=pltpu.CompilerParams(vmem_limit_bytes=GLUE_BYTES),
            name="feats",
        )(parts, mark)
    )
    other = lax.ppermute(own, "rep", [(0, 1), (1, 0)])

    step, down_step = chunk_rows(depth, 256), chunk_rows(latents, 256)
    partial, codes = pl.pallas_call(
        functools.partial(coder_kernel, rows, step, down_step),
        out_shape=(
            jax.ShapeDtypeStruct((n, out_share + 1, SUB, LANE), jnp.int16),
            jax.ShapeDtypeStruct((2 * slots, latents), BF),
        ),
        in_specs=[in_vmem, in_vmem, in_vmem, anywhere, anywhere],
        out_specs=(in_vmem, in_vmem),
        scratch_shapes=[
            pltpu.VMEM((depth, latents), F4),
            pltpu.VMEM((latents, width), F4),
            pltpu.VMEM((2 * rows, width), F4),
            pltpu.VMEM((slots, latents), F4),
            pltpu.VMEM((slots, width), F4),
            pltpu.SemaphoreType.DMA((depth // step + latents // down_step,)),
        ],
        compiler_params=pltpu.CompilerParams(vmem_limit_bytes=CODER_BYTES),
        name="coder",
    )(own, other, jnp.concatenate([enc_bias, dec_bias], axis=1), enc_weight, dec_weight)
    err = exchange(
        pl.pallas_call(
            functools.partial(err_kernel, across),
            out_shape=jax.ShapeDtypeStruct((n, out_share, SUB, LANE), BF),
            in_specs=[in_vmem],
            out_specs=in_vmem,
            compiler_params=pltpu.CompilerParams(vmem_limit_bytes=GLUE_BYTES),
            name="err",
        )(exchange(partial))
    )

    block = chunk_rows(latents, 128)
    return pl.pallas_call(
        functools.partial(grad_kernel, block),
        out_shape=jax.ShapeDtypeStruct((1, latents, width), F4),
        in_specs=[in_vmem, in_vmem],
        out_specs=anywhere,
        scratch_shapes=[
            pltpu.VMEM((2 * slots, width), BF),
            pltpu.VMEM((latents, width), F4),
            pltpu.SemaphoreType.DMA((latents // block,)),
        ],
        compiler_params=pltpu.CompilerParams(vmem_limit_bytes=GRAD_BYTES),
        name="grad",
    )(err, codes)


def solution(mesh):
    placed = (
        P(("groups", "lat", "rep"), None),
        P(("groups", "lat", "rep")),
        P(("groups", "lat", "rep")),
        P(None, "lat"),
        P(None, "lat"),
        P("lat", None),
        P("rep", None, "lat"),
        P("rep", "lat"),
        P("rep", "lat", None),
        P("rep", None),
    )
    return jax.shard_map(
        shards,
        mesh=mesh,
        in_specs=placed,
        out_specs=P(("groups", "rep"), "lat", None),
        check_vma=False,
    )
```

```python
import functools

import jax
import jax.numpy as jnp
from jax import lax
from jax.experimental import pallas as pl
from jax.experimental.pallas import tpu as pltpu
from jax.sharding import PartitionSpec as P

MB_REP = 4
CAP = 6
SUB = 8
LANE = 128
LIMIT = 32767.0
BF = jnp.bfloat16
F4 = jnp.float32
CODER_BYTES = 46 << 20
GRAD_BYTES = 26 << 20
GLUE_BYTES = 2 << 20
MLP_BYTES = 8 << 20


def dot(a, b):
    return jnp.dot(a, b, preferred_element_type=F4)


def split(x):
    high = x.astype(BF)
    return high, (x - high.astype(F4)).astype(BF)


def chunk_rows(extent, want):
    return want if extent % want == 0 else extent


def encode(local, out):
    share = out.shape[1] - 1
    across = local.shape[1] // LANE
    groups = local.shape[0] // SUB
    peak = jnp.max(jnp.abs(local), axis=1, keepdims=True)
    power = jnp.clip(jnp.ceil(jnp.log2(jnp.maximum(peak, 1e-30))), -96.0, 120.0)
    codes = jnp.clip(jnp.round(local * jnp.exp2(15.0 - power)), -LIMIT, LIMIT).astype(jnp.int32)
    lane = lax.broadcasted_iota(jnp.int32, (SUB, LANE), 1)
    powers = jnp.zeros((SUB, LANE), F4)
    for g in range(groups):
        powers = jnp.where(lane == g, power[g * SUB : (g + 1) * SUB], powers)
    powers = powers.astype(jnp.int32).astype(jnp.int16)
    for t in range(out.shape[0] * share):
        if t < groups * across:
            g, j = divmod(t, across)
            out[t // share, t % share] = codes[g * SUB : (g + 1) * SUB, j * LANE : (j + 1) * LANE].astype(jnp.int16)
        else:
            out[t // share, t % share] = jnp.zeros((SUB, LANE), jnp.int16)
    for s in range(out.shape[0]):
        out[s, share] = powers


def decode(parts, across):
    n, share = parts.shape[0], parts.shape[1] - 1
    start = lax.axis_index("lat") * share
    first = lax.div(start, across)
    lane = lax.broadcasted_iota(jnp.int32, (SUB, LANE), 1)
    units = []
    for s in range(n):
        scale = jnp.exp2(parts[s, share].astype(jnp.int32).astype(F4) - 15.0)
        units.append(
            [
                jnp.broadcast_to(jnp.sum(jnp.where(lane == first + h, scale, 0.0), axis=1, keepdims=True), (SUB, LANE))
                for h in range((share + across - 2) // across + 1)
            ]
        )
    tiles = []
    for t in range(share):
        ahead = lax.div(start + t, across) - first
        total = None
        for s in range(n):
            unit = units[s][0]
            for h in range(1, len(units[s])):
                unit = jnp.where(ahead == h, units[s][h], unit)
            value = parts[s, t].astype(jnp.int32).astype(F4) * unit
            total = value if total is None else total + value
        tiles.append(total.astype(BF))
    return tiles


def spread_kernel(acts, *rest):
    out = rest[-1]
    for s in range(out.shape[0]):
        out[s] = acts[...]


def feats_kernel(across, row_dev, parts, mark, out):
    tiles = decode(parts, across)
    turn = lax.broadcasted_iota(jnp.int32, (SUB, LANE), 0) // row_dev
    mine = turn == lax.rem(lax.axis_index("lat"), SUB // row_dev)
    tags = jnp.where(mine, mark[...], 0.0).astype(BF)
    for s in range(parts.shape[0]):
        for t, tile in enumerate(tiles):
            out[s, t] = tile
        out[s, len(tiles)] = tags


def err_kernel(across, parts, out):
    tiles = decode(parts, across)
    for s in range(parts.shape[0]):
        for t, tile in enumerate(tiles):
            out[s, t] = tile


def mlp_kernel(piece, gate_w, up_w, down_w, out):
    left = jnp.concatenate([piece[s].astype(F4) for s in range(piece.shape[0])], axis=0).astype(BF)
    gate = dot(left, gate_w[...])
    up = dot(left, up_w[...])
    hidden = (jax.nn.gelu(gate, approximate=True) * up).astype(BF)
    encode(dot(hidden, down_w[...]), out)


def coder_kernel(
    rows_side, step, down_step,
    own, other, biases, enc_hbm, dec_hbm,
    partial, codes_out,
    enc_v, dec_v, feats, acc, recon, sems,
):
    depth, latents = enc_v.shape
    width = dec_v.shape[1]
    across = width // LANE
    slots = acc.shape[0]
    encs, decs = [], []
    for k in range(depth // step):
        part = pl.ds(k * step, step)
        encs.append(pltpu.make_async_copy(enc_hbm.at[0, part], enc_v.at[part], sems.at[k]))
    for k in range(latents // down_step):
        part = pl.ds(k * down_step, down_step)
        decs.append(pltpu.make_async_copy(dec_hbm.at[0, part], dec_v.at[part], sems.at[len(encs) + k]))
    for copy in encs + decs:
        copy.start()

    share = own.shape[1] - 1
    labels = []
    for side, source in enumerate((own, other)):
        for g in range(rows_side // SUB):
            labels.append(source[2 * g, share].astype(F4) + source[2 * g + 1, share].astype(F4))
            for j in range(across):
                t = g * across + j
                feats[side * rows_side + g * SUB : side * rows_side + (g + 1) * SUB, j * LANE : (j + 1) * LANE] = source[t // share, t % share].astype(F4)
    label = jnp.concatenate(labels, axis=0)
    every = label.shape[0]
    first = (lax.axis_index("rep") * MB_REP).astype(F4) + 1.0
    keep = jnp.where((label >= first) & (label < first + MB_REP), 1.0, 0.0)
    row_of = lax.broadcasted_iota(jnp.int32, (every, every), 0)
    column_of = lax.broadcasted_iota(jnp.int32, (every, every), 1)
    keep_wide = jnp.broadcast_to(keep[:, :1], (every, every))
    keep_row = jnp.sum(jnp.where(row_of == column_of, keep_wide, 0.0), axis=0, keepdims=True)
    before = jnp.sum(jnp.where(row_of < column_of, keep_wide, 0.0), axis=0, keepdims=True)
    slot_of = lax.broadcasted_iota(jnp.int32, (slots, every), 0).astype(F4)
    picked = jnp.where((before == slot_of) & (keep_row > 0.0), 1.0, 0.0).astype(BF)
    slot_label = dot(picked, label.astype(BF))
    weight = jnp.zeros_like(slot_label)
    for m in range(MB_REP):
        size = jnp.sum(jnp.where(label == first + m, 1.0, 0.0), axis=0, keepdims=True)
        weight = weight + jnp.where(slot_label == first + m, 1.0 / jnp.maximum(size, 1.0), 0.0)
    twice = 2.0 * weight[:, :1]
    batch = dot(picked, feats[...].astype(BF))
    feats[0:slots, :] = batch

    for k, copy in enumerate(encs):
        left = batch[:, k * step : (k + 1) * step].astype(BF)
        copy.wait()
        high, low = split(enc_v[pl.ds(k * step, step), :])
        part = dot(left, high) + dot(left, low)
        if k == 0:
            acc[...] = part + biases[:, :latents]
        else:
            acc[...] += part
    codes = jnp.maximum(acc[...], 0.0)
    code_high, code_low = split(codes)
    out_high, out_low = split(twice * codes)
    codes_out[0:slots, :] = out_high
    codes_out[slots : 2 * slots, :] = out_low
    stacked = jnp.concatenate([code_high, code_low], axis=0)
    for k, copy in enumerate(decs):
        part = slice(k * down_step, (k + 1) * down_step)
        copy.wait()
        high, low = split(dec_v[pl.ds(k * down_step, down_step), :])
        both = dot(stacked[:, part], high)
        here = both[:slots] + both[slots:] + dot(code_high[:, part], low)
        if k == 0:
            recon[...] = here
        else:
            recon[...] += here
    leads = lax.axis_index("lat") == 0
    local = recon[...] + jnp.where(leads, biases[:, latents:] - feats[0:slots, :], 0.0)
    encode(local, partial)


def grad_kernel(block, err, codes, out, stacked, held, sems):
    slots = stacked.shape[0] // 2
    latents, width = held.shape
    across = width // LANE
    share = err.shape[1]
    for t in range(slots // SUB * across):
        g, j = divmod(t, across)
        tile = err[t // share, t % share]
        for half in (0, slots):
            stacked[half + g * SUB : half + (g + 1) * SUB, j * LANE : (j + 1) * LANE] = tile
    copies = []
    for k in range(latents // block):
        part = pl.ds(k * block, block)
        held[part, :] = lax.dot_general(
            codes[:, k * block : (k + 1) * block], stacked[...], (((0,), (0,)), ((), ())), preferred_element_type=F4
        )
        copies.append(pltpu.make_async_copy(held.at[part], out.at[0, part], sems.at[k]))
        copies[-1].start()
    for copy in copies:
        copy.wait()


def exchange(blocks):
    return lax.all_to_all(blocks, "lat", 0, 0)


def shards(acts, dest, counts, w_gate, w_up, w_down, enc_weight, enc_bias, dec_weight, dec_bias):
    n = lax.axis_size("lat")
    row_dev, depth = acts.shape
    hidden_n = w_gate.shape[1]
    width = w_down.shape[1]
    latents = enc_weight.shape[2]
    across = width // LANE
    rows = n * row_dev
    share = rows // SUB * across // n
    slots = n * CAP
    out_share = pl.cdiv(slots // SUB * across, n)
    anywhere = pl.BlockSpec(memory_space=pl.ANY)
    in_vmem = pl.BlockSpec(memory_space=pltpu.VMEM)

    ahead = [pltpu.with_memory_space_constraint(w, pltpu.HBM) for w in (enc_weight, dec_weight)]
    piece = exchange(
        pl.pallas_call(
            spread_kernel,
            out_shape=jax.ShapeDtypeStruct((n, row_dev, depth), BF),
            in_specs=[in_vmem] + [pl.BlockSpec(memory_space=pltpu.HBM)] * len(ahead),
            out_specs=in_vmem,
            compiler_params=pltpu.CompilerParams(vmem_limit_bytes=GLUE_BYTES),
            name="spread",
        )(acts, *ahead)
    )
    summed = pl.pallas_call(
        mlp_kernel,
        out_shape=jax.ShapeDtypeStruct((n, share + 1, SUB, LANE), jnp.int16),
        in_specs=[in_vmem] * 4,
        out_specs=in_vmem,
        compiler_params=pltpu.CompilerParams(vmem_limit_bytes=MLP_BYTES),
        name="mlp",
    )(piece, w_gate, w_up, w_down)
    parts = exchange(summed)

    tags = jnp.where(jnp.arange(row_dev, dtype=jnp.int32) < counts[0], dest + 1, 0)
    mark = jnp.broadcast_to(jnp.tile(tags, SUB // row_dev)[:, None], (SUB, LANE)).astype(F4)
    own = exchange(
        pl.pallas_call(
            functools.partial(feats_kernel, across, row_dev),
            out_shape=jax.ShapeDtypeStruct((n, share + 1, SUB, LANE), BF),
            in_specs=[in_vmem, in_vmem],
            out_specs=in_vmem,
            compiler_params=pltpu.CompilerParams(vmem_limit_bytes=GLUE_BYTES),
            name="feats",
        )(parts, mark)
    )
    other = lax.ppermute(own, "rep", [(0, 1), (1, 0)])

    step, down_step = chunk_rows(depth, 256), chunk_rows(latents, 256)
    partial, codes = pl.pallas_call(
        functools.partial(coder_kernel, rows, step, down_step),
        out_shape=(
            jax.ShapeDtypeStruct((n, out_share + 1, SUB, LANE), jnp.int16),
            jax.ShapeDtypeStruct((2 * slots, latents), BF),
        ),
        in_specs=[in_vmem, in_vmem, in_vmem, anywhere, anywhere],
        out_specs=(in_vmem, in_vmem),
        scratch_shapes=[
            pltpu.VMEM((depth, latents), F4),
            pltpu.VMEM((latents, width), F4),
            pltpu.VMEM((2 * rows, width), F4),
            pltpu.VMEM((slots, latents), F4),
            pltpu.VMEM((slots, width), F4),
            pltpu.SemaphoreType.DMA((depth // step + latents // down_step,)),
        ],
        compiler_params=pltpu.CompilerParams(vmem_limit_bytes=CODER_BYTES),
        name="coder",
    )(own, other, jnp.concatenate([enc_bias, dec_bias], axis=1), enc_weight, dec_weight)
    err = exchange(
        pl.pallas_call(
            functools.partial(err_kernel, across),
            out_shape=jax.ShapeDtypeStruct((n, out_share, SUB, LANE), BF),
            in_specs=[in_vmem],
            out_specs=in_vmem,
            compiler_params=pltpu.CompilerParams(vmem_limit_bytes=GLUE_BYTES),
            name="err",
        )(exchange(partial))
    )

    block = chunk_rows(latents, 128)
    return pl.pallas_call(
        functools.partial(grad_kernel, block),
        out_shape=jax.ShapeDtypeStruct((1, latents, width), F4),
        in_specs=[in_vmem, in_vmem],
        out_specs=anywhere,
        scratch_shapes=[
            pltpu.VMEM((2 * slots, width), BF),
            pltpu.VMEM((latents, width), F4),
            pltpu.SemaphoreType.DMA((latents // block,)),
        ],
        compiler_params=pltpu.CompilerParams(vmem_limit_bytes=GRAD_BYTES),
        name="grad",
    )(err, codes)


def solution(mesh):
    placed = (
        P(("groups", "lat", "rep"), None),
        P(("groups", "lat", "rep")),
        P(("groups", "lat", "rep")),
        P(None, "lat"),
        P(None, "lat"),
        P("lat", None),
        P("rep", None, "lat"),
        P("rep", "lat"),
        P("rep", "lat", None),
        P("rep", None),
    )
    return jax.shard_map(
        shards,
        mesh=mesh,
        in_specs=placed,
        out_specs=P(("groups", "rep"), "lat", None),
        check_vma=False,
    )
```
